32 devices in a mesh: blk: 32 (over z, y, x, core).
Axes of the slice: x: 2, y: 2, z: 4, core: 2. Of those that a mesh axis runs over, the one named last changes fastest.
Arguments:
- old_phase: float32 [512, 32768], P('blk'), may hold values from -1 to 1
- old_solute: float32 [512, 32768], P('blk'), may hold values from -0.45 to 0.45
- old_mobility: float32 [512, 32768], P('blk'), may hold values from 0.25 to 1
- new_global_slot: int32 [512], P('blk'), may hold values from -1 to 255, as said below
- neighbors: int32 [256, 6], P('blk'), may hold values from -1 to 255, as said below
Outputs:
- phase: float32 [256, 32768], P('blk')
- solute: float32 [256, 32768], P('blk')
The draws below stay inside these ranges and needn't reach their ends.
Inputs may be any that keep to these rules, and one draw needn't show every extreme that they name: Each device's old slots hold its blocks first and -1 after them; the blocks taken in device order and slot order get the consecutive numbers 0 to 255. The block in an old slot of device p goes to device new_global_slot // 8, at most 2 devices away; in every draw some block moves exactly 2 devices down and some exactly 2 up, some device holds 16 blocks and some none. `neighbors`: the relation is symmetric: if b is the +x (+y, +z) neighbour of a, then a is the -x (-y, -z) neighbour of b. The x neighbours of a block of device p lie on devices p - 1 and p + 1 (every block has both except on the first and last device, where that side is -1); y and z neighbours lie on the block's own device, with -1 at the ends along y and none along z (a block may be its own z neighbour). The layers of blocks line up: if b is the -x (+x) neighbour of a, then the y and z neighbours of b are the -x (+x) neighbours of the y and z neighbours of a, and -1 where those are -1.
All inputs are finite; a program needn't handle non-finite values.
Results may differ from the reference program's by a relative error of at most 0.00014.
Values sent between devices are 32-bit elements; how exact they have to be, the bound alone decides.
A program may use at most 128 MiB of HBM per device.

```python
import math
import jax
import jax.numpy as jnp
from jax import lax

BLOCK_EDGE_CELLS = 32
BLOCK_CELLS = 32768
FACE_CELLS = 1024
CAP = 8
SPREAD = 2
STEPS = 3
ACTIVE_BLOCKS = 256
NOLD = 512
N_BLK = 32


def draw_old_phase(key, part):
    cell_ids = jnp.arange(BLOCK_CELLS)
    xs = (cell_ids // FACE_CELLS).astype(jnp.float32)
    ys = (cell_ids // BLOCK_EDGE_CELLS % BLOCK_EDGE_CELLS).astype(jnp.float32)
    zs = (cell_ids % BLOCK_EDGE_CELLS).astype(jnp.float32)
    middle = (BLOCK_EDGE_CELLS - 1) / 2.0
    inverse_width = 1.0 / (math.sqrt(2.0) * BLOCK_EDGE_CELLS / 8.0)
    rough = jax.random.uniform(jax.random.fold_in(key, 31), (NOLD, BLOCK_CELLS), jnp.float32, -1.0, 1.0)
    azimuth = jax.random.uniform(jax.random.fold_in(key, 34), (NOLD, 1), jnp.float32, 0.0, 2.0 * math.pi)
    polar = jax.random.uniform(jax.random.fold_in(key, 35), (NOLD, 1), jnp.float32, 0.0, math.pi)
    shift_along = jax.random.uniform(jax.random.fold_in(key, 36), (NOLD, 1), jnp.float32, -BLOCK_EDGE_CELLS / 4.0, BLOCK_EDGE_CELLS / 4.0)
    normal_x = jnp.cos(azimuth) * jnp.sin(polar)
    normal_y = jnp.sin(azimuth) * jnp.sin(polar)
    normal_z = jnp.cos(polar)
    distance = normal_x * (xs[None, :] - middle) + normal_y * (ys[None, :] - middle) + normal_z * (zs[None, :] - middle) - shift_along
    phase = 0.92 * jnp.tanh(distance * inverse_width) + 0.08 * rough
    return phase.astype(jnp.float32)


def draw_new_global_slot(key, part):
    groups = N_BLK // (2 * SPREAD)
    depth = jax.random.randint(jax.random.fold_in(key, 1), (groups, SPREAD), 0, CAP + 1)
    flips = jax.random.randint(jax.random.fold_in(key, 2), (groups,), 0, 2)
    first = jax.random.randint(jax.random.fold_in(key, 3), (), 0, groups - 1)
    second = groups - 1
    group_ids = jnp.arange(groups)
    forced = (group_ids == first) | (group_ids == second)
    depth = jnp.where(forced[:, None], CAP, depth)
    flips = jnp.where(group_ids == first, 0, jnp.where(group_ids == second, 1, flips))
    signs = 1 - 2 * flips
    lower = CAP - signs[:, None] * depth
    upper = CAP + signs[:, None] * depth[:, ::-1]
    counts = jnp.concatenate([lower, upper], axis=1).reshape(N_BLK)
    starts = jnp.cumsum(counts) - counts
    slot_ids = jnp.arange(2 * CAP)
    result = jnp.where(slot_ids[None, :] < counts[:, None], starts[:, None] + slot_ids[None, :], -1)
    return result.reshape(NOLD).astype(jnp.int32)


def device_perms(key):
    return jax.vmap(lambda sub: jax.random.permutation(sub, CAP))(jax.random.split(key, N_BLK))


def draw_neighbors(key, part):
    columns = max(1, min(2, CAP // 2))
    rows_y = CAP // columns
    dev_ids = jnp.arange(N_BLK)[:, None]
    position = device_perms(jax.random.fold_in(key, 11))
    inverse = jnp.argsort(position, axis=1)
    prev_inverse = jnp.concatenate([inverse[:1], inverse[:-1]], axis=0)
    next_inverse = jnp.concatenate([inverse[1:], inverse[-1:]], axis=0)
    row_pos = position // columns
    col_pos = position % columns
    minus_x = jnp.where(dev_ids > 0, (dev_ids - 1) * CAP + jnp.take_along_axis(prev_inverse, position, axis=1), -1)
    plus_x = jnp.where(dev_ids < N_BLK - 1, (dev_ids + 1) * CAP + jnp.take_along_axis(next_inverse, position, axis=1), -1)
    here = dev_ids * CAP
    minus_y = jnp.where(row_pos > 0, here + jnp.take_along_axis(inverse, jnp.clip(position - columns, 0, CAP - 1), axis=1), -1)
    plus_y = jnp.where(row_pos < rows_y - 1, here + jnp.take_along_axis(inverse, jnp.clip(position + columns, 0, CAP - 1), axis=1), -1)
    minus_z = here + jnp.take_along_axis(inverse, row_pos * columns + (col_pos + columns - 1) % columns, axis=1)
    plus_z = here + jnp.take_along_axis(inverse, row_pos * columns + (col_pos + 1) % columns, axis=1)
    lookup_table = jnp.stack([minus_x, plus_x, minus_y, plus_y, minus_z, plus_z], axis=-1)
    return lookup_table.reshape(ACTIVE_BLOCKS, 6).astype(jnp.int32)


def shard_levels(own_key, shape, pieces, least, largest):
    factor_of, own = 1.0, jax.random.fold_in(own_key, 6)
    for dim, blocks in pieces:
        heights = jnp.exp(jax.random.uniform(jax.random.fold_in(own, dim), (blocks,), jnp.float32, least / len(pieces), largest / len(pieces)))
        factor_of = factor_of * jnp.repeat(heights, shape[dim] // blocks).reshape([-1 if axis == dim else 1 for axis in range(len(shape))])
    return factor_of


def noise(own_key, extent, width, limit, pieces=(), held_as=jnp.bfloat16):
    factor_of = shard_levels(own_key, extent, pieces, -0.22, 0.18) if pieces else 1.0
    array = jax.random.normal(own_key, extent, jnp.float32) * width * factor_of
    return jnp.minimum(jnp.maximum(array, -limit), limit).astype(held_as)


def setup_inputs(seed: int = 0) -> dict:
    key_of = jax.random.split(jax.random.key(seed), 6)
    return {
        "old_phase": draw_old_phase(jax.random.fold_in(key_of[5], 71), 0),
        "old_solute": noise(key_of[1], (NOLD, BLOCK_CELLS), 0.15, 0.45, ((0, 32),), jnp.float32),
        "old_mobility": jnp.clip(jnp.exp(math.log(1.0) - 1.3862944 * jax.random.uniform(key_of[2], (NOLD, BLOCK_CELLS), jnp.float32) ** shard_levels(key_of[2], (NOLD, BLOCK_CELLS), ((0, 32),), -0.2, 0.2)), 0.25, 1.0),
        "new_global_slot": draw_new_global_slot(jax.random.fold_in(key_of[5], 71), 0),
        "neighbors": draw_neighbors(jax.random.fold_in(key_of[5], 71), 0),
    }


time_step = 0.15
coupling = 1.5


def block_faces(field_arrays):
    edge = field_arrays.shape[2]
    low_x = field_arrays[:, :, 0, :]
    high_x = field_arrays[:, :, edge - 1, :]
    low_y = field_arrays[:, :, :, :edge]
    high_y = field_arrays[:, :, :, -edge:]
    low_z = field_arrays[:, :, :, 0::edge]
    high_z = field_arrays[:, :, :, edge - 1::edge]
    return low_x, high_x, low_y, high_y, low_z, high_z


def pick_face(other, own, index):
    valid = index >= 0
    taken = jnp.take(other, jnp.maximum(index, 0), axis=0)
    return jnp.where(valid.reshape((-1,) + (1,) * (own.ndim - 1)), taken, own)


def laplacian(field_arrays, ghosts):
    minus_x, plus_x, minus_y, plus_y, minus_z, plus_z = ghosts
    edge = field_arrays.shape[2]
    flat_ids = jnp.arange(field_arrays.shape[3], dtype=jnp.int32)
    y_ids = flat_ids // edge
    z_ids = flat_ids % edge
    prev_x = jnp.concatenate([minus_x[:, :, None, :], field_arrays[:, :, :-1, :]], axis=2)
    next_x = jnp.concatenate([field_arrays[:, :, 1:, :], plus_x[:, :, None, :]], axis=2)
    zero_row = jnp.zeros(field_arrays.shape[:3] + (edge,), jnp.float32)
    zero_one = jnp.zeros(field_arrays.shape[:3] + (1,), jnp.float32)
    prev_y = jnp.where(y_ids == 0, jnp.tile(minus_y, (1, 1, 1, edge)),
                       jnp.concatenate([zero_row, field_arrays[..., :-edge]], axis=-1))
    next_y = jnp.where(y_ids == edge - 1, jnp.tile(plus_y, (1, 1, 1, edge)),
                       jnp.concatenate([field_arrays[..., edge:], zero_row], axis=-1))
    prev_z = jnp.where(z_ids == 0, jnp.repeat(minus_z, edge, axis=-1),
                       jnp.concatenate([zero_one, field_arrays[..., :-1]], axis=-1))
    next_z = jnp.where(z_ids == edge - 1, jnp.repeat(plus_z, edge, axis=-1),
                       jnp.concatenate([field_arrays[..., 1:], zero_one], axis=-1))
    return (prev_x + next_x) + (prev_y + next_y) + (prev_z + next_z) - 6.0 * field_arrays


def advance(field_arrays, mobility, ghosts):
    lapl = laplacian(field_arrays, ghosts)
    phi = field_arrays[:, 0]
    conc = field_arrays[:, 1]
    wetting = 1.0 - phi * phi
    drive = lapl[:, 0] + phi - phi * phi * phi - coupling * conc * wetting * wetting
    new_phi = phi + time_step * mobility * drive
    new_conc = conc + time_step * lapl[:, 1] + 0.5 * (new_phi - phi)
    return jnp.stack([new_phi, new_conc], axis=1)


def reference(old_phase, old_solute, old_mobility, new_global_slot, neighbors):
    stacked_fields = jnp.stack([old_phase, old_solute, old_mobility], axis=1)
    target_slot = jnp.where(new_global_slot >= 0, new_global_slot, ACTIVE_BLOCKS).astype(jnp.int32)
    placed_blocks = jnp.zeros((ACTIVE_BLOCKS, 3, BLOCK_CELLS), jnp.float32).at[target_slot].set(stacked_fields, mode="drop")
    placed_blocks = placed_blocks.reshape(ACTIVE_BLOCKS, 3, BLOCK_EDGE_CELLS, FACE_CELLS)
    field_arrays = placed_blocks[:, :2]
    mobility = placed_blocks[:, 2]
    for step in range(STEPS):
        low_x, high_x, low_y, high_y, low_z, high_z = block_faces(field_arrays)
        ghosts = (pick_face(high_x, low_x, neighbors[:, 0]), pick_face(low_x, high_x, neighbors[:, 1]),
                  pick_face(high_y, low_y, neighbors[:, 2]), pick_face(low_y, high_y, neighbors[:, 3]),
                  pick_face(high_z, low_z, neighbors[:, 4]), pick_face(low_z, high_z, neighbors[:, 5]))
        grouped = jax.tree.map(lambda a: a.reshape((N_BLK, CAP) + a.shape[1:]), (field_arrays, mobility, ghosts))
        result = lax.map(lambda t: advance(t[0], t[1], t[2]), grouped)
        field_arrays = result.reshape(field_arrays.shape)
    return field_arrays[:, 0].reshape(ACTIVE_BLOCKS, BLOCK_CELLS), field_arrays[:, 1].reshape(ACTIVE_BLOCKS, BLOCK_CELLS)
```

```python
import functools

import jax
import jax.numpy as jnp
from jax import lax
from jax.experimental import pallas as pl
from jax.experimental.pallas import tpu as pltpu
from jax.sharding import PartitionSpec as P

EDGE = 32
STEPS = 3
FIELDS = 3
SUB = 8
LANES = 128
LAG = 3

time_step = 0.15
coupling = 1.5


def kernel(n, cap, nold, ngs, nbs, op, oc, om, phi_out, conc_out, old,
           side_s, side_r, pair_s, pair_r, far_s, far_r, near_s, near_r,
           fld, mob, ghost0, ghost1, ghost2, lsem, ssem, rsem, hs, hr):
    ghosts = (ghost0, ghost1, ghost2)
    rows = EDGE * SUB
    span = nold * rows
    items = FIELDS * cap
    loads = [
        pltpu.make_async_copy(src, old.at[pl.ds(f * span, span)], lsem.at[f])
        for f, src in enumerate((op, oc, om))
    ]
    for copy in loads:
        copy.start()

    me = lax.axis_index("blk")
    core = me % 2
    odd = (me // 2) % 2
    sib = me + 1 - 2 * core
    near = me + 2 - 4 * odd
    far_final = me - 2 + 4 * odd
    far = (me + n - 4 + 8 * odd) % n
    side_final = me - 1 + 2 * core
    up = (me + 1) % n
    down = (me + n - 1) % n

    barrier = pltpu.get_barrier_semaphore()
    partners = (up, down, near, (me + 4) % n, (me + n - 4) % n)
    for other in partners:
        pl.semaphore_signal(barrier, inc=1, device_id=(other,), device_id_type=pl.DeviceIdType.MESH)

    start = ngs[0]
    count = jnp.int32(0)
    for s in range(nold):
        count = count + (ngs[s] >= 0).astype(jnp.int32)

    def held(i, final):
        f, j = lax.div(i, cap), lax.rem(i, cap)
        idx = final * cap + j - start
        mine = (idx >= 0) & (idx < count)
        idx = jnp.clip(idx, 0, nold - 1)
        row = f * span + lax.div(idx, SUB) * (rows * SUB) + lax.rem(idx, SUB)
        got = old[pl.ds(row, rows, stride=SUB), :]
        return jnp.where(mine, got, 0.0).reshape(EDGE, SUB, LANES)

    def link(stream, src, dst, i, target):
        return pltpu.make_async_remote_copy(
            src_ref=src.at[i], dst_ref=dst.at[i],
            send_sem=ssem.at[stream, i], recv_sem=rsem.at[stream, i],
            device_id=(target,), device_id_type=pl.DeviceIdType.MESH)

    def side_link(i):
        return link(0, side_s, side_r, i, sib)

    def pair_link(i):
        return link(1, pair_s, pair_r, i, sib)

    def far_link(i):
        return link(2, far_s, far_r, i, far)

    def near_link(i):
        return link(3, near_s, near_r, i, near)

    side_goes_far = (core + odd) % 2 == 1

    def send_side(i):
        side_s[i] = held(i, side_final)
        side_link(i).start()

    def send_pair(i):
        pair_s[i] = held(i, sib)
        pair_link(i).start()

    def send_far(i):
        side_link(i).wait_recv()
        far_s[i] = held(i, far_final) + jnp.where(side_goes_far, side_r[i], 0.0)
        far_link(i).start()

    def send_near(i):
        far_link(i).wait_recv()
        near_s[i] = held(i, near) + (far_r[i] + jnp.where(side_goes_far, 0.0, side_r[i]))
        near_link(i).start()

    def loop(lo, hi, *bodies):
        def body(i, carry):
            for each in bodies:
                each(i)
            return carry
        lax.fori_loop(lo, hi, body, 0)

    for copy in loads:
        copy.wait()
    pl.semaphore_wait(barrier, len(partners))
    loop(0, items, send_side)
    loop(0, LAG, send_far)
    loop(LAG, items, send_far, lambda i: send_near(i - LAG))
    loop(items - LAG, items, send_near)
    loop(0, items, send_pair)

    def settle(i):
        pair_link(i).wait_recv()
        near_link(i).wait_recv()
        return held(i, me) + (pair_r[i] + near_r[i])

    def settle_field(i):
        fld[0, lax.div(i, cap), lax.rem(i, cap)] = settle(i)

    def settle_mobility(i):
        mob[i - 2 * cap] = settle(i)

    def ghost_links(t):
        return (
            pltpu.make_async_remote_copy(
                src_ref=fld.at[t, :, :, EDGE - 1], dst_ref=ghosts[t].at[0],
                send_sem=hs.at[t, 0], recv_sem=hr.at[t, 0],
                device_id=(up,), device_id_type=pl.DeviceIdType.MESH),
            pltpu.make_async_remote_copy(
                src_ref=fld.at[t, :, :, 0], dst_ref=ghosts[t].at[1],
                send_sem=hs.at[t, 1], recv_sem=hr.at[t, 1],
                device_id=(down,), device_id_type=pl.DeviceIdType.MESH),
        )

    loop(0, 2 * cap, settle_field)
    for copy in ghost_links(0):
        copy.start()
    loop(2 * cap, items, settle_mobility)

    lane = lax.broadcasted_iota(jnp.int32, (SUB, LANES), 1)
    row = lax.broadcasted_iota(jnp.int32, (SUB, LANES), 0)
    z = lane % EDGE
    z_low, z_high = z == 0, z == EDGE - 1
    y_first, y_last = lane < EDGE, lane >= LANES - EDGE
    row_first, row_last = row == 0, row == SUB - 1

    def local(column, b):
        index = nbs[b * 6 + column]
        return lax.rem(jnp.maximum(index, 0), cap), index >= 0

    def advance(t, b, planes):
        at_y0, has_y0 = local(2, b)
        at_y1, has_y1 = local(3, b)
        at_z0, has_z0 = local(4, b)
        at_z1, has_z1 = local(5, b)
        wall_y0 = y_first & row_first & jnp.logical_not(has_y0)
        wall_y1 = y_last & row_last & jnp.logical_not(has_y1)
        wall_z0 = z_low & jnp.logical_not(has_z0)
        wall_z1 = z_high & jnp.logical_not(has_z1)

        def laplacian(f, x, prev_x, here, next_x):
            y0, y1 = fld[t, f, at_y0, x], fld[t, f, at_y1, x]
            z0, z1 = fld[t, f, at_z0, x], fld[t, f, at_z1, x]
            back = pltpu.roll(here, EDGE, 1)
            back_ghost = pltpu.roll(y0, EDGE, 1)
            prev_y = jnp.where(y_first, pltpu.roll(jnp.where(row_last, back_ghost, back), 1, 0), back)
            prev_y = jnp.where(wall_y0, here, prev_y)
            fore = pltpu.roll(here, LANES - EDGE, 1)
            fore_ghost = pltpu.roll(y1, LANES - EDGE, 1)
            next_y = jnp.where(y_last, pltpu.roll(jnp.where(row_first, fore_ghost, fore), SUB - 1, 0), fore)
            next_y = jnp.where(wall_y1, here, next_y)
            prev_z = jnp.where(z_low, pltpu.roll(z0, LANES - (EDGE - 1), 1), pltpu.roll(here, 1, 1))
            prev_z = jnp.where(wall_z0, here, prev_z)
            next_z = jnp.where(z_high, pltpu.roll(z1, EDGE - 1, 1), pltpu.roll(here, LANES - 1, 1))
            next_z = jnp.where(wall_z1, here, next_z)
            return (prev_x + next_x) + (prev_y + next_y) + (prev_z + next_z) - 6.0 * here

        for x, beside in planes:
            phi, conc = fld[t, 0, b, x], fld[t, 1, b, x]
            lapl_phi = laplacian(0, x, beside(0)[0], phi, beside(0)[1])
            lapl_conc = laplacian(1, x, beside(1)[0], conc, beside(1)[1])
            wetting = 1.0 - phi * phi
            drive = lapl_phi + phi - phi * phi * phi - coupling * conc * wetting * wetting
            new_phi = phi + time_step * mob[b, x] * drive
            new_conc = conc + time_step * lapl_conc + 0.5 * (new_phi - phi)
            if t == STEPS - 1:
                at = lax.div(b, SUB) * (rows * SUB) + lax.rem(b, SUB) + x * (SUB * SUB)
                phi_out[pl.ds(at, SUB, stride=SUB), :] = new_phi
                conc_out[pl.ds(at, SUB, stride=SUB), :] = new_conc
            else:
                fld[t + 1, 0, b, x] = new_phi
                fld[t + 1, 1, b, x] = new_conc

    inner = 3 if (EDGE - 2) % 3 == 0 else 1
    for t in range(STEPS):
        for copy in ghost_links(t):
            copy.wait_recv()

        def ends(b):
            at_x0, has_x0 = local(0, b)
            at_x1, has_x1 = local(1, b)

            def low(f):
                return (jnp.where(has_x0, ghosts[t][0, f, at_x0], fld[t, f, b, 0]), fld[t, f, b, 1])

            def high(f):
                return (fld[t, f, b, EDGE - 2],
                        jnp.where(has_x1, ghosts[t][1, f, at_x1], fld[t, f, b, EDGE - 1]))

            advance(t, b, ((0, low), (EDGE - 1, high)))

        def middle(b):
            def some(k, carry):
                planes = []
                for u in range(inner):
                    x = 1 + k * inner + u
                    planes.append((x, lambda f, x=x: (fld[t, f, b, x - 1], fld[t, f, b, x + 1])))
                advance(t, b, planes)
                return carry
            lax.fori_loop(0, (EDGE - 2) // inner, some, 0)

        loop(0, cap, ends)
        if t + 1 < STEPS:
            for copy in ghost_links(t + 1):
                copy.start()
        loop(0, cap, middle)

    def sent(i):
        side_link(i).wait_send()
        pair_link(i).wait_send()
        far_link(i).wait_send()
        near_link(i).wait_send()

    loop(0, items, sent)
    for t in range(STEPS):
        for copy in ghost_links(t):
            copy.wait_send()


def on_device(n, old_phase, old_solute, old_mobility, new_global_slot, neighbors):
    cap = neighbors.shape[0]
    nold, cells = old_phase.shape
    rows = cells // LANES
    items = FIELDS * cap

    def tiled(field):
        split = field.reshape(nold // SUB, SUB, rows, LANES)
        return split.transpose(0, 2, 1, 3).reshape(nold * rows, LANES)

    def flat(field):
        split = field.reshape(cap // SUB, rows, SUB, LANES)
        return split.transpose(0, 2, 1, 3).reshape(cap, cells)

    buffer = pltpu.VMEM((items, EDGE, SUB, LANES), jnp.float32)
    out = jax.ShapeDtypeStruct((cap * rows, LANES), jnp.float32)
    phase, solute = pl.pallas_call(
        functools.partial(kernel, n, cap, nold),
        out_shape=(out, out),
        in_specs=[pl.BlockSpec(memory_space=pltpu.SMEM)] * 2 + [pl.BlockSpec(memory_space=pl.ANY)] * 3,
        out_specs=[pl.BlockSpec(memory_space=pltpu.VMEM)] * 2,
        scratch_shapes=[pltpu.VMEM((FIELDS * nold * rows, LANES), jnp.float32)] + [buffer] * 8 + [
            pltpu.VMEM((STEPS, 2, cap, EDGE, SUB, LANES), jnp.float32),
            pltpu.VMEM((cap, EDGE, SUB, LANES), jnp.float32),
        ] + [pltpu.VMEM((2, 2, cap, SUB, LANES), jnp.float32)] * STEPS + [
            pltpu.SemaphoreType.DMA((FIELDS,)),
            pltpu.SemaphoreType.DMA((4, items)),
            pltpu.SemaphoreType.DMA((4, items)),
            pltpu.SemaphoreType.DMA((STEPS, 2)),
            pltpu.SemaphoreType.DMA((STEPS, 2)),
        ],
        compiler_params=pltpu.CompilerParams(
            collective_id=0, has_side_effects=True, vmem_limit_bytes=56 * 1024 * 1024),
    )(new_global_slot, neighbors.reshape(-1), tiled(old_phase), tiled(old_solute), tiled(old_mobility))
    return flat(phase), flat(solute)


def solution(mesh):
    placed = (P("blk", None), P("blk", None), P("blk", None), P("blk"), P("blk", None))
    return jax.shard_map(
        functools.partial(on_device, mesh.shape["blk"]),
        mesh=mesh,
        in_specs=placed,
        out_specs=(P("blk", None), P("blk", None)),
        check_vma=False,
    )
```

```python
import functools

import jax
import jax.numpy as jnp
from jax import lax
from jax.experimental import pallas as pl
from jax.experimental.pallas import tpu as pltpu
from jax.sharding import PartitionSpec as P

EDGE = 32
STEPS = 3
FIELDS = 3
SUB = 8
LANES = 128
LAG = 3
AHEAD = 2
INNER = 5

time_step = 0.15
coupling = 1.5


def kernel(n, cap, nold, ngs, nbs, op, oc, om, phi_out, conc_out, old,
           side_s, side_r, pair_s, pair_r, far_s, far_r, near_s, near_r,
           fld0, fld1, fld2, mob, ghost0, ghost1, ghost2, lsem, ssem, rsem, hs, hr):
    flds = (fld0, fld1, fld2)
    ghosts = (ghost0, ghost1, ghost2)
    rows = EDGE * SUB
    span = nold * rows
    items = FIELDS * cap
    loads = [
        pltpu.make_async_copy(src, old.at[pl.ds(f * span, span)], lsem.at[f])
        for f, src in enumerate((op, oc, om))
    ]
    for copy in loads:
        copy.start()

    me = lax.axis_index("blk")
    core = me % 2
    odd = (me // 2) % 2
    sib = me + 1 - 2 * core
    near = me + 2 - 4 * odd
    far_final = me - 2 + 4 * odd
    far = (me + n - 4 + 8 * odd) % n
    side_final = me - 1 + 2 * core
    up = (me + 1) % n
    down = (me + n - 1) % n

    barrier = pltpu.get_barrier_semaphore()
    partners = (up, down, near, (me + 4) % n, (me + n - 4) % n)
    for other in partners:
        pl.semaphore_signal(barrier, inc=1, device_id=(other,), device_id_type=pl.DeviceIdType.MESH)

    start = ngs[0]
    count = jnp.int32(0)
    for s in range(nold):
        count = count + (ngs[s] >= 0).astype(jnp.int32)

    def held(i, final):
        f, j = lax.div(i, cap), lax.rem(i, cap)
        idx = final * cap + j - start
        mine = (idx >= 0) & (idx < count)
        idx = jnp.clip(idx, 0, nold - 1)
        row = f * span + lax.div(idx, SUB) * (rows * SUB) + lax.rem(idx, SUB)
        got = old[pl.ds(row, rows, stride=SUB), :]
        return jnp.where(mine, got, 0.0).reshape(EDGE, SUB, LANES)

    def link(stream, src, dst, i, target):
        return pltpu.make_async_remote_copy(
            src_ref=src.at[i], dst_ref=dst.at[i],
            send_sem=ssem.at[stream, i], recv_sem=rsem.at[stream, i],
            device_id=(target,), device_id_type=pl.DeviceIdType.MESH)

    def side_link(i):
        return link(0, side_s, side_r, i, sib)

    def pair_link(i):
        return link(1, pair_s, pair_r, i, sib)

    def far_link(i):
        return link(2, far_s, far_r, i, far)

    def near_link(i):
        return link(3, near_s, near_r, i, near)

    side_goes_far = (core + odd) % 2 == 1

    def send_side(i):
        side_s[i] = held(i, side_final)
        side_link(i).start()

    def send_pair(i):
        pair_s[i] = held(i, sib)
        pair_link(i).start()

    def send_far(i):
        side_link(i).wait_recv()
        far_s[i] = held(i, far_final) + jnp.where(side_goes_far, side_r[i], 0.0)
        far_link(i).start()

    def send_near(i):
        far_link(i).wait_recv()
        near_s[i] = held(i, near) + (far_r[i] + jnp.where(side_goes_far, 0.0, side_r[i]))
        near_link(i).start()

    def loop(lo, hi, *bodies):
        def body(i, carry):
            for each in bodies:
                each(i)
            return carry
        lax.fori_loop(lo, hi, body, 0)

    def pipeline(stages, hooks):
        cuts = set(hooks)
        for _, offset, size in stages:
            cuts |= {offset, offset + size}
        cuts = sorted(cuts)
        for lo, hi in zip(cuts, cuts[1:] + cuts[-1:]):
            for act in hooks.get(lo, ()):
                act()
            active = [(body, offset) for body, offset, size in stages if offset <= lo and hi <= offset + size]
            if lo < hi and active:
                loop(lo, hi, *[lambda i, body=body, offset=offset: body(i - offset) for body, offset in active])

    def settle(i):
        pair_link(i).wait_recv()
        near_link(i).wait_recv()
        return held(i, me) + (pair_r[i] + near_r[i])

    def settle_field(i):
        flds[0][lax.div(i, cap), lax.rem(i, cap)] = settle(i)

    def settle_mobility(b):
        mobility = settle(b + 2 * cap)
        mob[b] = mobility
        phi = flds[0][0, b]
        new_phi = phi + time_step * mobility * flds[1][0, b]
        flds[1][0, b] = new_phi
        flds[1][1, b] = flds[1][1, b] + 0.5 * (new_phi - phi)

    def ghost_links(t):
        return (
            pltpu.make_async_remote_copy(
                src_ref=flds[t].at[:, :, EDGE - 1], dst_ref=ghosts[t].at[0],
                send_sem=hs.at[t, 0], recv_sem=hr.at[t, 0],
                device_id=(up,), device_id_type=pl.DeviceIdType.MESH),
            pltpu.make_async_remote_copy(
                src_ref=flds[t].at[:, :, 0], dst_ref=ghosts[t].at[1],
                send_sem=hs.at[t, 1], recv_sem=hr.at[t, 1],
                device_id=(down,), device_id_type=pl.DeviceIdType.MESH),
        )

    def start_ghosts(t):
        for copy in ghost_links(t):
            copy.start()

    def await_ghosts(t):
        for copy in ghost_links(t):
            copy.wait_recv()

    lane = lax.broadcasted_iota(jnp.int32, (SUB, LANES), 1)
    row = lax.broadcasted_iota(jnp.int32, (SUB, LANES), 0)
    z = lane % EDGE
    z_low, z_high = z == 0, z == EDGE - 1
    y_first, y_last = lane < EDGE, lane >= LANES - EDGE
    y_start, y_end = y_first & (row == 0), y_last & (row == SUB - 1)

    def local(column, b):
        index = nbs[b, column]
        return lax.rem(jnp.maximum(index, 0), cap), index >= 0

    def advance(t, b, planes):
        fld = flds[t]
        at_y0, has_y0 = local(2, b)
        at_y1, has_y1 = local(3, b)
        at_z0, _ = local(4, b)
        at_z1, _ = local(5, b)
        wall_y0 = y_start & jnp.logical_not(has_y0)
        wall_y1 = y_end & jnp.logical_not(has_y1)

        def laplacian(f, x, prev_x, here, next_x):
            y0, y1 = fld[f, at_y0, x], fld[f, at_y1, x]
            z0, z1 = fld[f, at_z0, x], fld[f, at_z1, x]
            back = pltpu.roll(jnp.where(y_end, y0, here), EDGE, 1)
            prev_y = jnp.where(y_first, pltpu.roll(back, 1, 0), back)
            prev_y = jnp.where(wall_y0, here, prev_y)
            fore = pltpu.roll(jnp.where(y_start, y1, here), LANES - EDGE, 1)
            next_y = jnp.where(y_last, pltpu.roll(fore, SUB - 1, 0), fore)
            next_y = jnp.where(wall_y1, here, next_y)
            prev_z = jnp.where(z_low, pltpu.roll(z0, LANES - (EDGE - 1), 1), pltpu.roll(here, 1, 1))
            next_z = jnp.where(z_high, pltpu.roll(z1, EDGE - 1, 1), pltpu.roll(here, LANES - 1, 1))
            return (prev_x + next_x) + (prev_y + next_y) + (prev_z + next_z) - 6.0 * here

        results = []
        for x, beside in planes:
            phi, conc = fld[0, b, x], fld[1, b, x]
            lapl_phi = laplacian(0, x, beside(0)[0], phi, beside(0)[1])
            lapl_conc = laplacian(1, x, beside(1)[0], conc, beside(1)[1])
            wetting = 1.0 - phi * phi
            drive = lapl_phi + phi - phi * phi * phi - coupling * conc * wetting * wetting
            new_conc = conc + time_step * lapl_conc
            if t == 0:
                results.append((x, drive, new_conc))
                continue
            new_phi = phi + time_step * mob[b, x] * drive
            results.append((x, new_phi, new_conc + 0.5 * (new_phi - phi)))
        for x, new_phi, new_conc in results:
            if t == STEPS - 1:
                at = lax.div(b, SUB) * (rows * SUB) + lax.rem(b, SUB) + x * (SUB * SUB)
                phi_out[pl.ds(at, SUB, stride=SUB), :] = new_phi
                conc_out[pl.ds(at, SUB, stride=SUB), :] = new_conc
            else:
                flds[t + 1][0, b, x] = new_phi
                flds[t + 1][1, b, x] = new_conc

    inner = max(k for k in range(1, INNER + 1) if (EDGE - 2) % k == 0)

    def ends(t, b):
        at_x0, has_x0 = local(0, b)
        at_x1, has_x1 = local(1, b)
        fld = flds[t]

        def low(f):
            return (jnp.where(has_x0, ghosts[t][0, f, at_x0], fld[f, b, 0]), fld[f, b, 1])

        def high(f):
            return (fld[f, b, EDGE - 2], jnp.where(has_x1, ghosts[t][1, f, at_x1], fld[f, b, EDGE - 1]))

        advance(t, b, ((0, low), (EDGE - 1, high)))

    def middle(t, b):
        fld = flds[t]

        def some(k, carry):
            planes = []
            for u in range(inner):
                x = 1 + k * inner + u
                planes.append((x, lambda f, x=x: (fld[f, b, x - 1], fld[f, b, x + 1])))
            advance(t, b, planes)
            return carry
        lax.fori_loop(0, (EDGE - 2) // inner, some, 0)

    def prepare(b):
        ends(0, b)
        middle(0, b)

    for copy in loads:
        copy.wait()
    pl.semaphore_wait(barrier, len(partners))
    far_at = AHEAD
    near_at = far_at + LAG
    settle_at = near_at + LAG + 1
    ghosts_at = settle_at + 2 * cap
    pipeline(
        (
            (send_side, 0, items),
            (send_far, far_at, items),
            (send_near, near_at, items),
            (send_pair, near_at, items),
            (settle_field, settle_at, 2 * cap),
        ),
        {ghosts_at: (lambda: start_ghosts(0),)},
    )
    await_ghosts(0)
    loop(0, cap, prepare)
    loop(0, cap, settle_mobility)
    start_ghosts(1)
    for t in range(1, STEPS):
        loop(0, cap, functools.partial(middle, t))
        await_ghosts(t)
        loop(0, cap, functools.partial(ends, t))
        if t + 1 < STEPS:
            start_ghosts(t + 1)

    def sent(i):
        side_link(i).wait_send()
        pair_link(i).wait_send()
        far_link(i).wait_send()
        near_link(i).wait_send()

    loop(0, items, sent)
    for t in range(STEPS):
        for copy in ghost_links(t):
            copy.wait_send()


def on_device(n, old_phase, old_solute, old_mobility, new_global_slot, neighbors):
    cap = neighbors.shape[0]
    nold, cells = old_phase.shape
    rows = cells // LANES
    items = FIELDS * cap

    def tiled(field):
        split = field.reshape(nold // SUB, SUB, rows, LANES)
        return split.transpose(0, 2, 1, 3).reshape(nold * rows, LANES)

    def flat(field):
        split = field.reshape(cap // SUB, rows, SUB, LANES)
        return split.transpose(0, 2, 1, 3).reshape(cap, cells)

    buffer = pltpu.VMEM((items, EDGE, SUB, LANES), jnp.float32)
    out = jax.ShapeDtypeStruct((cap * rows, LANES), jnp.float32)
    phase, solute = pl.pallas_call(
        functools.partial(kernel, n, cap, nold),
        out_shape=(out, out),
        in_specs=[pl.BlockSpec(memory_space=pltpu.SMEM)] * 2 + [pl.BlockSpec(memory_space=pl.ANY)] * 3,
        out_specs=[pl.BlockSpec(memory_space=pltpu.VMEM)] * 2,
        scratch_shapes=[pltpu.VMEM((FIELDS * nold * rows, LANES), jnp.float32)] + [buffer] * 8 + [
            pltpu.VMEM((2, cap, EDGE, SUB, LANES), jnp.float32)] * STEPS + [
            pltpu.VMEM((cap, EDGE, SUB, LANES), jnp.float32),
        ] + [pltpu.VMEM((2, 2, cap, SUB, LANES), jnp.float32)] * STEPS + [
            pltpu.SemaphoreType.DMA((FIELDS,)),
            pltpu.SemaphoreType.DMA((4, items)),
            pltpu.SemaphoreType.DMA((4, items)),
            pltpu.SemaphoreType.DMA((STEPS, 2)),
            pltpu.SemaphoreType.DMA((STEPS, 2)),
        ],
        compiler_params=pltpu.CompilerParams(
            collective_id=0, has_side_effects=True, vmem_limit_bytes=56 * 1024 * 1024),
    )(new_global_slot, neighbors, tiled(old_phase), tiled(old_solute), tiled(old_mobility))
    return flat(phase), flat(solute)


def solution(mesh):
    placed = (P("blk", None), P("blk", None), P("blk", None), P("blk"), P("blk", None))
    return jax.shard_map(
        functools.partial(on_device, mesh.shape["blk"]),
        mesh=mesh,
        in_specs=placed,
        out_specs=(P("blk", None), P("blk", None)),
        check_vma=False,
    )
```

```python
import functools

import jax
import jax.numpy as jnp
from jax import lax
from jax.experimental import pallas as pl
from jax.experimental.pallas import tpu as pltpu
from jax.sharding import PartitionSpec as P

EDGE = 32
STEPS = 3
FIELDS = 3
SUB = 8
LANES = 128
PARTS = 2
LAG = 4
AHEAD = 2
SETTLE = 4
INNER = 10

time_step = 0.15
coupling = 1.5


def kernel(n, cap, nold, ngs, nbs, op, oc, om, phi_out, conc_out, old,
           side_s, side_r, pair_s, pair_r, far_s, far_r, near_s, near_r,
           fld0, fld1, fld2, mob, ghost0, ghost1, ghost2, lsem, ssem, rsem, hs, hr):
    flds = (fld0, fld1, fld2)
    ghosts = (ghost0, ghost1, ghost2)
    rows = EDGE * SUB
    span = nold * rows
    part = rows // PARTS
    items = FIELDS * cap * PARTS
    loads = [
        pltpu.make_async_copy(src, old.at[pl.ds(f * span, span)], lsem.at[f])
        for f, src in enumerate((op, oc, om))
    ]
    for copy in loads:
        copy.start()

    me = lax.axis_index("blk")
    core = me % 2
    odd = (me // 2) % 2
    sib = me + 1 - 2 * core
    near = me + 2 - 4 * odd
    far_final = me - 2 + 4 * odd
    far = me - 4 + 8 * odd
    far_source = me + 4 - 8 * odd
    side_final = me - 1 + 2 * core
    up, down = me + 1, me - 1
    has_up, has_down = up < n, down >= 0
    sends_far = (far_final >= 0) & (far_final < n)
    gets_far = (far_source >= 0) & (far_source < n)

    barrier = pltpu.get_barrier_semaphore()
    expected = jnp.int32(0)
    for other, there in ((up, has_up), (down, has_down), (near, None), (far, sends_far), (far_source, gets_far)):
        def greet(other=other):
            pl.semaphore_signal(barrier, inc=1, device_id=(other,), device_id_type=pl.DeviceIdType.MESH)
        if there is None:
            greet()
            expected = expected + 1
        else:
            pl.when(there)(greet)
            expected = expected + there.astype(jnp.int32)

    start = ngs[0]
    count = jnp.int32(0)
    for s in range(nold):
        count = count + (ngs[s] >= 0).astype(jnp.int32)

    def place(i):
        block = lax.div(i, PARTS)
        return lax.div(block, cap), lax.rem(block, cap), lax.rem(i, PARTS)

    def held(i, final):
        f, j, h = place(i)
        idx = final * cap + j - start
        mine = (idx >= 0) & (idx < count)
        idx = jnp.clip(idx, 0, nold - 1)
        row = f * span + lax.div(idx, SUB) * (rows * SUB) + lax.rem(idx, SUB) + h * (part * SUB)
        got = old[pl.ds(row, part, stride=SUB), :]
        return jnp.where(mine, got, 0.0).reshape(EDGE // PARTS, SUB, LANES)

    def link(stream, src, dst, i, target):
        return pltpu.make_async_remote_copy(
            src_ref=src.at[i], dst_ref=dst.at[i],
            send_sem=ssem.at[stream, i], recv_sem=rsem.at[stream, i],
            device_id=(target,), device_id_type=pl.DeviceIdType.MESH)

    def side_link(i):
        return link(0, side_s, side_r, i, sib)

    def pair_link(i):
        return link(1, pair_s, pair_r, i, sib)

    def far_link(i):
        return link(2, far_s, far_r, i, far)

    def near_link(i):
        return link(3, near_s, near_r, i, near)

    side_goes_far = (core + odd) % 2 == 1

    def send_side(i):
        side_s[i] = held(i, side_final)
        side_link(i).start()

    def send_pair(i):
        pair_s[i] = held(i, sib)
        pair_link(i).start()

    def add_side(i, total):
        side_link(i).wait_recv()
        total[i] += side_r[i]

    def send_far(i):
        far_s[i] = held(i, far_final)
        pl.when(side_goes_far)(lambda: add_side(i, far_s))
        pl.when(sends_far)(lambda: far_link(i).start())

    def send_near(i):
        near_s[i] = held(i, near)
        pl.when(jnp.logical_not(side_goes_far))(lambda: add_side(i, near_s))

        @pl.when(gets_far)
        def add_far():
            far_link(i).wait_recv()
            near_s[i] += far_r[i]

        near_link(i).start()

    def loop(lo, hi, *bodies):
        def body(i, carry):
            for each in bodies:
                each(i)
            return carry
        lax.fori_loop(lo, hi, body, 0)

    def pipeline(stages, hooks):
        cuts = set(hooks)
        for _, offset, size in stages:
            cuts |= {offset, offset + size}
        cuts = sorted(cuts)
        for lo, hi in zip(cuts, cuts[1:] + cuts[-1:]):
            for act in hooks.get(lo, ()):
                act()
            active = [(body, offset) for body, offset, size in stages if offset <= lo and hi <= offset + size]
            if lo < hi and active:
                loop(lo, hi, *[lambda i, body=body, offset=offset: body(i - offset) for body, offset in active])

    def settle(i):
        pair_link(i).wait_recv()
        near_link(i).wait_recv()
        return held(i, me) + (pair_r[i] + near_r[i])

    def settle_field(i):
        f, j, h = place(i)
        planes = pl.ds(h * (EDGE // PARTS), EDGE // PARTS)
        flds[0][f, j, planes] = settle(i)

    def settle_mobility(i):
        _, b, h = place(i)
        planes = pl.ds(h * (EDGE // PARTS), EDGE // PARTS)
        mobility = settle(i + 2 * cap * PARTS)
        mob[b, planes] = mobility
        phi = flds[0][0, b, planes]
        new_phi = phi + time_step * mobility * flds[1][0, b, planes]
        flds[1][0, b, planes] = new_phi
        flds[1][1, b, planes] = flds[1][1, b, planes] + 0.5 * (new_phi - phi)

    def ghost_link(t, side):
        return pltpu.make_async_remote_copy(
            src_ref=flds[t].at[:, :, 0 if side else EDGE - 1], dst_ref=ghosts[t].at[side],
            send_sem=hs.at[t, side], recv_sem=hr.at[t, side],
            device_id=(down if side else up,), device_id_type=pl.DeviceIdType.MESH)

    def start_ghosts(t):
        pl.when(has_up)(lambda: ghost_link(t, 0).start())
        pl.when(has_down)(lambda: ghost_link(t, 1).start())

    def await_ghosts(t):
        pl.when(has_down)(lambda: ghost_link(t, 0).wait_recv())
        pl.when(has_up)(lambda: ghost_link(t, 1).wait_recv())

    def await_sent(t):
        pl.when(has_up)(lambda: ghost_link(t, 0).wait_send())
        pl.when(has_down)(lambda: ghost_link(t, 1).wait_send())

    lane = lax.broadcasted_iota(jnp.int32, (SUB, LANES), 1)
    row = lax.broadcasted_iota(jnp.int32, (SUB, LANES), 0)
    z = lane % EDGE
    z_low, z_high = z == 0, z == EDGE - 1
    y_first, y_last = lane < EDGE, lane >= LANES - EDGE
    y_start, y_end = y_first & (row == 0), y_last & (row == SUB - 1)

    def local(column, b):
        index = nbs[b, column]
        return lax.rem(jnp.maximum(index, 0), cap), index >= 0

    def advance(t, b, planes):
        fld = flds[t]
        at_y0, has_y0 = local(2, b)
        at_y1, has_y1 = local(3, b)
        at_z0, _ = local(4, b)
        at_z1, _ = local(5, b)
        wall_y0 = y_start & jnp.logical_not(has_y0)
        wall_y1 = y_end & jnp.logical_not(has_y1)

        def laplacian(f, x, prev_x, here, next_x):
            y0, y1 = fld[f, at_y0, x], fld[f, at_y1, x]
            z0, z1 = fld[f, at_z0, x], fld[f, at_z1, x]
            back = pltpu.roll(jnp.where(y_end, y0, here), EDGE, 1)
            prev_y = jnp.where(y_first, pltpu.roll(back, 1, 0), back)
            prev_y = jnp.where(wall_y0, here, prev_y)
            fore = pltpu.roll(jnp.where(y_start, y1, here), LANES - EDGE, 1)
            next_y = jnp.where(y_last, pltpu.roll(fore, SUB - 1, 0), fore)
            next_y = jnp.where(wall_y1, here, next_y)
            prev_z = jnp.where(z_low, pltpu.roll(z0, LANES - (EDGE - 1), 1), pltpu.roll(here, 1, 1))
            next_z = jnp.where(z_high, pltpu.roll(z1, EDGE - 1, 1), pltpu.roll(here, LANES - 1, 1))
            return (prev_x + next_x) + (prev_y + next_y) + (prev_z + next_z) - 6.0 * here

        results = []
        for x, beside in planes:
            phi, conc = fld[0, b, x], fld[1, b, x]
            lapl_phi = laplacian(0, x, beside(0)[0], phi, beside(0)[1])
            lapl_conc = laplacian(1, x, beside(1)[0], conc, beside(1)[1])
            wetting = 1.0 - phi * phi
            drive = lapl_phi + phi - phi * phi * phi - coupling * conc * wetting * wetting
            new_conc = conc + time_step * lapl_conc
            if t == 0:
                results.append((x, drive, new_conc))
                continue
            new_phi = phi + time_step * mob[b, x] * drive
            results.append((x, new_phi, new_conc + 0.5 * (new_phi - phi)))
        for x, new_phi, new_conc in results:
            if t == STEPS - 1:
                at = lax.div(b, SUB) * (rows * SUB) + lax.rem(b, SUB) + x * (SUB * SUB)
                phi_out[pl.ds(at, SUB, stride=SUB), :] = new_phi
                conc_out[pl.ds(at, SUB, stride=SUB), :] = new_conc
            else:
                flds[t + 1][0, b, x] = new_phi
                flds[t + 1][1, b, x] = new_conc

    inner = max(k for k in range(1, INNER + 1) if (EDGE - 2) % k == 0)

    def ends(t, b):
        at_x0, has_x0 = local(0, b)
        at_x1, has_x1 = local(1, b)
        fld = flds[t]

        def low(f):
            return (jnp.where(has_x0, ghosts[t][0, f, at_x0], fld[f, b, 0]), fld[f, b, 1])

        def high(f):
            return (fld[f, b, EDGE - 2], jnp.where(has_x1, ghosts[t][1, f, at_x1], fld[f, b, EDGE - 1]))

        advance(t, b, ((0, low), (EDGE - 1, high)))

    def middle(t, b):
        fld = flds[t]

        def some(k, carry):
            planes = []
            for u in range(inner):
                x = 1 + k * inner + u
                planes.append((x, lambda f, x=x: (fld[f, b, x - 1], fld[f, b, x + 1])))
            advance(t, b, planes)
            return carry
        lax.fori_loop(0, (EDGE - 2) // inner, some, 0)

    def prepare(b):
        ends(0, b)
        middle(0, b)

    for copy in loads:
        copy.wait()
    pl.semaphore_wait(barrier, expected)
    fields = 2 * cap * PARTS
    near_at = AHEAD + LAG
    settle_at = near_at + SETTLE
    ghosts_at = settle_at + fields
    prepare_at = ghosts_at + 2
    pipeline(
        (
            (send_side, 0, items),
            (send_far, AHEAD, items),
            (send_near, near_at, items),
            (send_pair, near_at, items),
            (settle_field, settle_at, fields),
            (prepare, prepare_at, cap),
            (settle_mobility, prepare_at + 1, cap * PARTS),
        ),
        {ghosts_at: (lambda: start_ghosts(0),), prepare_at: (lambda: await_ghosts(0),)},
    )
    start_ghosts(1)
    for t in range(1, STEPS):
        loop(0, cap, functools.partial(middle, t))
        await_ghosts(t)
        loop(0, cap, functools.partial(ends, t))
        if t + 1 < STEPS:
            start_ghosts(t + 1)

    def sent(i):
        side_link(i).wait_send()
        pair_link(i).wait_send()
        pl.when(sends_far)(lambda: far_link(i).wait_send())
        near_link(i).wait_send()

    loop(0, items, sent)
    for t in range(STEPS):
        await_sent(t)


def on_device(n, old_phase, old_solute, old_mobility, new_global_slot, neighbors):
    cap = neighbors.shape[0]
    nold, cells = old_phase.shape
    rows = cells // LANES
    items = FIELDS * cap * PARTS

    def tiled(field):
        split = field.reshape(nold // SUB, SUB, rows, LANES)
        return split.transpose(0, 2, 1, 3).reshape(nold * rows, LANES)

    def flat(field):
        split = field.reshape(cap // SUB, rows, SUB, LANES)
        return split.transpose(0, 2, 1, 3).reshape(cap, cells)

    buffer = pltpu.VMEM((items, EDGE // PARTS, SUB, LANES), jnp.float32)
    out = jax.ShapeDtypeStruct((cap * rows, LANES), jnp.float32)
    phase, solute = pl.pallas_call(
        functools.partial(kernel, n, cap, nold),
        out_shape=(out, out),
        in_specs=[pl.BlockSpec(memory_space=pltpu.SMEM)] * 2 + [pl.BlockSpec(memory_space=pl.ANY)] * 3,
        out_specs=[pl.BlockSpec(memory_space=pltpu.VMEM)] * 2,
        scratch_shapes=[pltpu.VMEM((FIELDS * nold * rows, LANES), jnp.float32)] + [buffer] * 8 + [
            pltpu.VMEM((2, cap, EDGE, SUB, LANES), jnp.float32)] * STEPS + [
            pltpu.VMEM((cap, EDGE, SUB, LANES), jnp.float32),
        ] + [pltpu.VMEM((2, 2, cap, SUB, LANES), jnp.float32)] * STEPS + [
            pltpu.SemaphoreType.DMA((FIELDS,)),
            pltpu.SemaphoreType.DMA((4, items)),
            pltpu.SemaphoreType.DMA((4, items)),
            pltpu.SemaphoreType.DMA((STEPS, 2)),
            pltpu.SemaphoreType.DMA((STEPS, 2)),
        ],
        compiler_params=pltpu.CompilerParams(
            collective_id=0, has_side_effects=True, vmem_limit_bytes=56 * 1024 * 1024),
    )(new_global_slot, neighbors, tiled(old_phase), tiled(old_solute), tiled(old_mobility))
    return flat(phase), flat(solute)


def solution(mesh):
    placed = (P("blk", None), P("blk", None), P("blk", None), P("blk"), P("blk", None))
    return jax.shard_map(
        functools.partial(on_device, mesh.shape["blk"]),
        mesh=mesh,
        in_specs=placed,
        out_specs=(P("blk", None), P("blk", None)),
        check_vma=False,
    )
```

```python
import functools

import jax
import jax.numpy as jnp
from jax import lax
from jax.experimental import pallas as pl
from jax.experimental.pallas import tpu as pltpu
from jax.sharding import PartitionSpec as P

EDGE = 32
STEPS = 3
FIELDS = 3
SUB = 8
LANES = 128
PARTS = 1
LAG = 2
AHEAD = 2
SETTLE = 2
INNER = 15

time_step = 0.15
coupling = 1.5


def kernel(n, cap, nold, ngs, nbs, op, oc, om, phi_out, conc_out, old,
           side_s, side_r, pair_s, pair_r, far_s, far_r, near_s, near_r,
           fld0, fld1, fld2, mob, ghost0, ghost1, ghost2, lsem, ssem, rsem, hs, hr):
    flds = (fld0, fld1, fld2)
    ghosts = (ghost0, ghost1, ghost2)
    rows = EDGE * SUB
    span = nold * rows
    part = rows // PARTS
    items = FIELDS * cap * PARTS
    loads = [
        pltpu.make_async_copy(src, old.at[pl.ds(f * span, span)], lsem.at[f])
        for f, src in enumerate((op, oc, om))
    ]
    for copy in loads:
        copy.start()

    me = lax.axis_index("blk")
    core = me % 2
    odd = (me // 2) % 2
    sib = me + 1 - 2 * core
    near = me + 2 - 4 * odd
    far_final = me - 2 + 4 * odd
    far = me - 4 + 8 * odd
    far_source = me + 4 - 8 * odd
    side_final = me - 1 + 2 * core
    up, down = me + 1, me - 1
    has_up, has_down = up < n, down >= 0
    sends_far = (far_final >= 0) & (far_final < n)
    gets_far = (far_source >= 0) & (far_source < n)

    barrier = pltpu.get_barrier_semaphore()
    expected = jnp.int32(0)
    for other, there in ((up, has_up), (down, has_down), (near, None), (far, sends_far), (far_source, gets_far)):
        def greet(other=other):
            pl.semaphore_signal(barrier, inc=1, device_id=(other,), device_id_type=pl.DeviceIdType.MESH)
        if there is None:
            greet()
            expected = expected + 1
        else:
            pl.when(there)(greet)
            expected = expected + there.astype(jnp.int32)

    start = ngs[0]
    count = jnp.int32(0)
    for s in range(nold):
        count = count + (ngs[s] >= 0).astype(jnp.int32)

    def place(i):
        block = lax.div(i, PARTS)
        return lax.div(block, cap), lax.rem(block, cap), lax.rem(i, PARTS)

    def held(i, final):
        f, j, h = place(i)
        idx = final * cap + j - start
        mine = (idx >= 0) & (idx < count)
        idx = jnp.clip(idx, 0, nold - 1)
        row = f * span + lax.div(idx, SUB) * (rows * SUB) + lax.rem(idx, SUB) + h * (part * SUB)
        got = old[pl.ds(row, part, stride=SUB), :]
        return jnp.where(mine, got, 0.0).reshape(EDGE // PARTS, SUB, LANES)

    def link(stream, src, dst, i, target):
        return pltpu.make_async_remote_copy(
            src_ref=src.at[i], dst_ref=dst.at[i],
            send_sem=ssem.at[stream, i], recv_sem=rsem.at[stream, i],
            device_id=(target,), device_id_type=pl.DeviceIdType.MESH)

    def side_link(i):
        return link(0, side_s, side_r, i, sib)

    def pair_link(i):
        return link(1, pair_s, pair_r, i, sib)

    def far_link(i):
        return link(2, far_s, far_r, i, far)

    def near_link(i):
        return link(3, near_s, near_r, i, near)

    side_goes_far = (core + odd) % 2 == 1

    def send_side(i):
        side_s[i] = held(i, side_final)
        side_link(i).start()

    def send_pair(i):
        pair_s[i] = held(i, sib)
        pair_link(i).start()

    def add_side(i, total):
        side_link(i).wait_recv()
        total[i] += side_r[i]

    def send_far(i):
        far_s[i] = held(i, far_final)
        pl.when(side_goes_far)(lambda: add_side(i, far_s))
        pl.when(sends_far)(lambda: far_link(i).start())

    def send_near(i):
        near_s[i] = held(i, near)
        pl.when(jnp.logical_not(side_goes_far))(lambda: add_side(i, near_s))

        @pl.when(gets_far)
        def add_far():
            far_link(i).wait_recv()
            near_s[i] += far_r[i]

        near_link(i).start()

    def loop(lo, hi, *bodies):
        def body(i, carry):
            for each in bodies:
                each(i)
            return carry
        lax.fori_loop(lo, hi, body, 0)

    def pipeline(stages, hooks):
        cuts = set(hooks)
        for _, offset, size in stages:
            cuts |= {offset, offset + size}
        cuts = sorted(cuts)
        for lo, hi in zip(cuts, cuts[1:] + cuts[-1:]):
            for act in hooks.get(lo, ()):
                act()
            active = [(body, offset) for body, offset, size in stages if offset <= lo and hi <= offset + size]
            if lo < hi and active:
                loop(lo, hi, *[lambda i, body=body, offset=offset: body(i - offset) for body, offset in active])

    def settle(i):
        pair_link(i).wait_recv()
        near_link(i).wait_recv()
        return held(i, me) + (pair_r[i] + near_r[i])

    def settle_field(i):
        f, j, h = place(i)
        planes = pl.ds(h * (EDGE // PARTS), EDGE // PARTS)
        flds[0][f, j, planes] = settle(i)

    def settle_mobility(i):
        _, b, h = place(i)
        planes = pl.ds(h * (EDGE // PARTS), EDGE // PARTS)
        mobility = settle(i + 2 * cap * PARTS)
        mob[b, planes] = mobility
        phi = flds[0][0, b, planes]
        new_phi = phi + time_step * mobility * flds[1][0, b, planes]
        flds[1][0, b, planes] = new_phi
        flds[1][1, b, planes] = flds[1][1, b, planes] + 0.5 * (new_phi - phi)

    def ghost_link(t, side):
        return pltpu.make_async_remote_copy(
            src_ref=flds[t].at[:, :, 0 if side else EDGE - 1], dst_ref=ghosts[t].at[side],
            send_sem=hs.at[t, side], recv_sem=hr.at[t, side],
            device_id=(down if side else up,), device_id_type=pl.DeviceIdType.MESH)

    def start_ghosts(t):
        pl.when(has_up)(lambda: ghost_link(t, 0).start())
        pl.when(has_down)(lambda: ghost_link(t, 1).start())

    def await_ghosts(t):
        pl.when(has_down)(lambda: ghost_link(t, 0).wait_recv())
        pl.when(has_up)(lambda: ghost_link(t, 1).wait_recv())

    def await_sent(t):
        pl.when(has_up)(lambda: ghost_link(t, 0).wait_send())
        pl.when(has_down)(lambda: ghost_link(t, 1).wait_send())

    lane = lax.broadcasted_iota(jnp.int32, (SUB, LANES), 1)
    row = lax.broadcasted_iota(jnp.int32, (SUB, LANES), 0)
    z = lane % EDGE
    z_low, z_high = z == 0, z == EDGE - 1
    y_first, y_last = lane < EDGE, lane >= LANES - EDGE
    y_start, y_end = y_first & (row == 0), y_last & (row == SUB - 1)

    def local(column, b):
        index = nbs[b, column]
        return lax.rem(jnp.maximum(index, 0), cap), index >= 0

    def advance(t, b, planes):
        fld = flds[t]
        at_y0, has_y0 = local(2, b)
        at_y1, has_y1 = local(3, b)
        at_z0, _ = local(4, b)
        at_z1, _ = local(5, b)
        wall_y0 = y_start & jnp.logical_not(has_y0)
        wall_y1 = y_end & jnp.logical_not(has_y1)

        def laplacian(f, x, prev_x, here, next_x):
            y0, y1 = fld[f, at_y0, x], fld[f, at_y1, x]
            z0, z1 = fld[f, at_z0, x], fld[f, at_z1, x]
            back = pltpu.roll(jnp.where(y_end, y0, here), EDGE, 1)
            prev_y = jnp.where(y_first, pltpu.roll(back, 1, 0), back)
            prev_y = jnp.where(wall_y0, here, prev_y)
            fore = pltpu.roll(jnp.where(y_start, y1, here), LANES - EDGE, 1)
            next_y = jnp.where(y_last, pltpu.roll(fore, SUB - 1, 0), fore)
            next_y = jnp.where(wall_y1, here, next_y)
            prev_z = jnp.where(z_low, pltpu.roll(z0, LANES - (EDGE - 1), 1), pltpu.roll(here, 1, 1))
            next_z = jnp.where(z_high, pltpu.roll(z1, EDGE - 1, 1), pltpu.roll(here, LANES - 1, 1))
            return (prev_x + next_x) + (prev_y + next_y) + (prev_z + next_z) - 6.0 * here

        results = []
        for x, beside in planes:
            phi, conc = fld[0, b, x], fld[1, b, x]
            lapl_phi = laplacian(0, x, beside(0)[0], phi, beside(0)[1])
            lapl_conc = laplacian(1, x, beside(1)[0], conc, beside(1)[1])
            wetting = 1.0 - phi * phi
            drive = lapl_phi + phi - phi * phi * phi - coupling * conc * wetting * wetting
            new_conc = conc + time_step * lapl_conc
            if t == 0:
                results.append((x, drive, new_conc))
                continue
            new_phi = phi + time_step * mob[b, x] * drive
            results.append((x, new_phi, new_conc + 0.5 * (new_phi - phi)))
        for x, new_phi, new_conc in results:
            if t == STEPS - 1:
                at = lax.div(b, SUB) * (rows * SUB) + lax.rem(b, SUB) + x * (SUB * SUB)
                phi_out[pl.ds(at, SUB, stride=SUB), :] = new_phi
                conc_out[pl.ds(at, SUB, stride=SUB), :] = new_conc
            else:
                flds[t + 1][0, b, x] = new_phi
                flds[t + 1][1, b, x] = new_conc

    inner = max(k for k in range(1, INNER + 1) if (EDGE - 2) % k == 0)

    def ends(t, b):
        at_x0, has_x0 = local(0, b)
        at_x1, has_x1 = local(1, b)
        fld = flds[t]

        def low(f):
            return (jnp.where(has_x0, ghosts[t][0, f, at_x0], fld[f, b, 0]), fld[f, b, 1])

        def high(f):
            return (fld[f, b, EDGE - 2], jnp.where(has_x1, ghosts[t][1, f, at_x1], fld[f, b, EDGE - 1]))

        advance(t, b, ((0, low), (EDGE - 1, high)))

    def middle(t, b):
        fld = flds[t]

        def some(k, carry):
            planes = []
            for u in range(inner):
                x = 1 + k * inner + u
                planes.append((x, lambda f, x=x: (fld[f, b, x - 1], fld[f, b, x + 1])))
            advance(t, b, planes)
            return carry
        lax.fori_loop(0, (EDGE - 2) // inner, some, 0)

    def prepare(b):
        ends(0, b)
        middle(0, b)

    for copy in loads:
        copy.wait()
    pl.semaphore_wait(barrier, expected)
    fields = 2 * cap * PARTS
    near_at = AHEAD + LAG
    settle_at = near_at + SETTLE
    ghosts_at = settle_at + fields
    prepare_at = ghosts_at + 1
    pipeline(
        (
            (send_side, 0, items),
            (send_far, AHEAD, items),
            (send_near, near_at, items),
            (send_pair, near_at, items),
            (settle_field, settle_at, fields),
            (prepare, prepare_at, cap),
            (settle_mobility, prepare_at + 1, cap * PARTS),
        ),
        {ghosts_at: (lambda: start_ghosts(0),), prepare_at: (lambda: await_ghosts(0),)},
    )
    start_ghosts(1)
    for t in range(1, STEPS):
        loop(0, cap, functools.partial(middle, t))
        await_ghosts(t)
        loop(0, cap, functools.partial(ends, t))
        if t + 1 < STEPS:
            start_ghosts(t + 1)

    def sent(i):
        side_link(i).wait_send()
        pair_link(i).wait_send()
        pl.when(sends_far)(lambda: far_link(i).wait_send())
        near_link(i).wait_send()

    loop(0, items, sent)
    for t in range(STEPS):
        await_sent(t)


def on_device(n, old_phase, old_solute, old_mobility, new_global_slot, neighbors):
    cap = neighbors.shape[0]
    nold, cells = old_phase.shape
    rows = cells // LANES
    items = FIELDS * cap * PARTS

    def tiled(field):
        split = field.reshape(nold // SUB, SUB, rows, LANES)
        return split.transpose(0, 2, 1, 3).reshape(nold * rows, LANES)

    def flat(field):
        split = field.reshape(cap // SUB, rows, SUB, LANES)
        return split.transpose(0, 2, 1, 3).reshape(cap, cells)

    buffer = pltpu.VMEM((items, EDGE // PARTS, SUB, LANES), jnp.float32)
    out = jax.ShapeDtypeStruct((cap * rows, LANES), jnp.float32)
    phase, solute = pl.pallas_call(
        functools.partial(kernel, n, cap, nold),
        out_shape=(out, out),
        in_specs=[pl.BlockSpec(memory_space=pltpu.SMEM)] * 2 + [pl.BlockSpec(memory_space=pl.ANY)] * 3,
        out_specs=[pl.BlockSpec(memory_space=pltpu.VMEM)] * 2,
        scratch_shapes=[pltpu.VMEM((FIELDS * nold * rows, LANES), jnp.float32)] + [buffer] * 8 + [
            pltpu.VMEM((2, cap, EDGE, SUB, LANES), jnp.float32)] * STEPS + [
            pltpu.VMEM((cap, EDGE, SUB, LANES), jnp.float32),
        ] + [pltpu.VMEM((2, 2, cap, SUB, LANES), jnp.float32)] * STEPS + [
            pltpu.SemaphoreType.DMA((FIELDS,)),
            pltpu.SemaphoreType.DMA((4, items)),
            pltpu.SemaphoreType.DMA((4, items)),
            pltpu.SemaphoreType.DMA((STEPS, 2)),
            pltpu.SemaphoreType.DMA((STEPS, 2)),
        ],
        compiler_params=pltpu.CompilerParams(
            collective_id=0, has_side_effects=True, vmem_limit_bytes=56 * 1024 * 1024),
    )(new_global_slot, neighbors, tiled(old_phase), tiled(old_solute), tiled(old_mobility))
    return flat(phase), flat(solute)


def solution(mesh):
    placed = (P("blk", None), P("blk", None), P("blk", None), P("blk"), P("blk", None))
    return jax.shard_map(
        functools.partial(on_device, mesh.shape["blk"]),
        mesh=mesh,
        in_specs=placed,
        out_specs=(P("blk", None), P("blk", None)),
        check_vma=False,
    )
```
